128 devices in a mesh: row: 8 (over y, z_lo), col: 16 (over z_hi, x, core).
Axes of the slice: x: 4, y: 4, z: 4 (z_hi: 2, z_lo: 2; z = z_hi * 2 + z_lo), core: 2. Of those that a mesh axis runs over, the one named last changes fastest.
Arguments:
- kernel: bfloat16 [20480, 20480], P('row', 'col'), may hold values from -2.861023e-06 to 2.861023e-06
- occ: bfloat16 [20480, 128], P(('row', 'col')), may hold values from -6 to 6
- virt: bfloat16 [20480, 512], P(('col', 'row')), may hold values from -6 to 6
- rhs: float32 [128, 512], replicated, may hold values from -6 to 6
- e_occ: float32 [128], replicated, may hold values from -2 to -0.5
- e_virt: float32 [512], replicated, may hold values from 0.2 to 3
Outputs:
- amplitudes: float32 [128, 512], replicated
The draws below stay inside these ranges and needn't reach their ends.
All inputs are finite; a program needn't handle non-finite values.
Results may differ from the reference program's by a relative error of at most 0.0045.
Values may be sent and summed in bfloat16 or wider, within the bound.
No kernel may reach another device: no remote copies, remote signals or barrier semaphores. Data moves between devices by JAX's collectives and lax.ppermute only.
A program may use at most 64 MiB of HBM per device.

```python
import math
import jax
import jax.numpy as jnp
from jax import lax

NO = 128
NV = 512
ITERS = 2
PTS = 20480


def levels(rng, extent, pieces, smallest, top_value):
    factor_of = 1.0
    for position, shards_of in pieces:
        draws = jax.random.uniform(jax.random.fold_in(jax.random.fold_in(rng, 6), position), (shards_of,), jnp.float32, smallest / len(pieces), top_value / len(pieces))
        factor_of = factor_of * jnp.repeat(jnp.exp(draws), extent[position] // shards_of).reshape((-1,) + (1,) * (len(extent) - 1 - position))
    return factor_of


def normal_values(key, extent, width, most, cuts=(), dtype=jnp.bfloat16):
    gain = levels(key, extent, cuts, -0.22, 0.18) if cuts else 1.0
    drawn = jax.random.normal(key, extent, jnp.float32) * width * gain
    return jnp.minimum(jnp.maximum(drawn, -most), most).astype(dtype)


def setup_inputs(seed: int = 0) -> dict:
    keys = jax.random.split(jax.random.key(seed), 7)
    kernel = normal_values(keys[0], (PTS, PTS), ((NO * NV) ** -0.5 / PTS), 2.86102294921875e-06, ((0, 8), (1, 16)))
    occ = normal_values(keys[1], (PTS, NO), 1.0, 6.0, ((0, 128),))
    virt = normal_values(keys[2], (PTS, NV), 1.0, 6.0, ((0, 128),))
    rhs = normal_values(keys[3], (NO, NV), 1.0, 6.0, (), jnp.float32)
    e_occ = jnp.clip(jax.random.uniform(keys[4], (NO,), jnp.float32, -2.0, -0.5), -2.0, -0.5)
    e_virt = jnp.clip(jax.random.uniform(keys[5], (NV,), jnp.float32, 0.2, 3.0), 0.2, 3.0)
    return {"kernel": kernel, "occ": occ, "virt": virt, "rhs": rhs, "e_occ": e_occ, "e_virt": e_virt}


def reference(kernel, occ, virt, rhs, e_occ, e_virt):
    denom = e_virt[None, :] - e_occ[:, None]
    amplitudes = rhs / denom
    block = math.gcd(PTS, 1024)
    count = PTS // block
    for step in range(ITERS):
        amp_b = amplitudes.astype(jnp.bfloat16)
        resp = jnp.dot(occ, amp_b, preferred_element_type=jnp.float32).astype(jnp.bfloat16)

        def add_block(index, total):
            start = (index * block).astype(jnp.int32)
            resp_rows = lax.dynamic_slice_in_dim(resp, start, block, 0)
            occ_rows = lax.dynamic_slice_in_dim(occ, start, block, 0)
            kern_rows = lax.dynamic_slice_in_dim(kernel, start, block, 0)
            outer = lax.dot_general(resp_rows, virt, (((1,), (1,)), ((), ())), preferred_element_type=jnp.float32)
            weighted = (kern_rows.astype(jnp.float32) * outer).astype(jnp.bfloat16)
            return total + lax.dot_general(occ_rows, weighted, (((0,), (0,)), ((), ())), preferred_element_type=jnp.float32)

        contracted = lax.fori_loop(0, count, add_block, jnp.zeros((NO, PTS), jnp.float32))
        exchange = jnp.dot(contracted, virt.astype(jnp.float32), precision=lax.Precision.HIGHEST)
        amplitudes = (rhs - exchange) / denom
    return amplitudes
```

```python
import functools

import jax
import jax.numpy as jnp
from jax import lax
from jax.experimental import pallas as pl
from jax.experimental.pallas import tpu as pltpu
from jax.sharding import PartitionSpec as P

ITERS = 2
LANES = 128
BOTH = ("row", "col")


def sent_to_all(shard, axis):
    peers = lax.axis_size(axis)
    return lax.all_to_all(
        jnp.broadcast_to(shard[None], (peers, *shard.shape)), axis, 0, 0, tiled=True
    )


def gathered(shard, axis):
    pieces = sent_to_all(shard, axis)
    return pieces.reshape(pieces.shape[0] * pieces.shape[1], *pieces.shape[2:])


def response_kernel(wide, amp_ref, virt_ref, occ_ref, occ_t_ref, kern_ref, out_ref, w_ref, total_ref):
    step = pl.program_id(0)
    cols = virt_ref.shape[0]
    nt = (((1,), (1,)), ((), ()))
    f32, b16 = jnp.float32, jnp.bfloat16

    @pl.when(step == 0)
    def _():
        for start in range(0, cols, wide):
            here = pl.ds(start, wide)
            w_ref[:, here] = lax.dot_general(
                amp_ref[...], virt_ref[here, :], nt, preferred_element_type=f32
            ).astype(b16)
        total_ref[...] = jnp.zeros_like(total_ref)

    for start in range(0, cols, wide):
        here = pl.ds(start, wide)
        outer = jnp.dot(occ_ref[...], w_ref[:, here], preferred_element_type=f32)
        weighted = (kern_ref[:, here].astype(f32) * outer).astype(b16)
        total_ref[:, here] += jnp.dot(occ_t_ref[...], weighted, preferred_element_type=f32)

    @pl.when(step == pl.num_programs(0) - 1)
    def _():
        total = total_ref[...]
        high = total.astype(b16)
        low = (total - high.astype(f32)).astype(b16)
        exchange = jnp.dot(high, virt_ref[...], preferred_element_type=f32)
        exchange += jnp.dot(low, virt_ref[...], preferred_element_type=f32)
        out_ref[...] = exchange.astype(out_ref.dtype)


def partial_exchange(amp_b, virt_cols, occ_rows, occ_t, kernel):
    occupied, virtual = amp_b.shape
    rows, cols = kernel.shape
    height, wide = 512, 256
    whole = lambda *dims: pl.BlockSpec(dims, lambda s: (0, 0))
    return pl.pallas_call(
        functools.partial(response_kernel, wide),
        out_shape=jax.ShapeDtypeStruct((occupied, virtual), jnp.bfloat16),
        grid=(rows // height,),
        in_specs=[
            whole(occupied, virtual),
            whole(cols, virtual),
            pl.BlockSpec((height, occupied), lambda s: (s, 0)),
            pl.BlockSpec((occupied, height), lambda s: (0, s)),
            pl.BlockSpec((height, cols), lambda s: (s, 0)),
        ],
        out_specs=whole(occupied, virtual),
        scratch_shapes=[
            pltpu.VMEM((occupied, cols), jnp.bfloat16),
            pltpu.VMEM((occupied, cols), jnp.float32),
        ],
        compiler_params=pltpu.CompilerParams(
            dimension_semantics=("arbitrary",), vmem_limit_bytes=40 << 20
        ),
    )(amp_b, virt_cols, occ_rows, occ_t, kernel)


def body(kernel, occ, virt, rhs, e_occ, e_virt):
    occupied, virtual = rhs.shape
    split = (occupied, virtual // LANES, LANES)
    mine = lax.axis_index("row") * lax.axis_size("col") + lax.axis_index("col")
    virt_cols = gathered(virt, "row")
    occ_rows = gathered(occ, "col")
    occ_t = occ_rows.T
    rhs_mine = lax.dynamic_index_in_dim(rhs, mine, 0, False).reshape(split[1:])
    denom_mine = e_virt.reshape(split[1:]) - lax.dynamic_index_in_dim(e_occ, mine, 0, False)

    amp_b = (rhs / (e_virt[None, :] - e_occ[:, None])).astype(jnp.bfloat16)
    for step in range(ITERS):
        part = partial_exchange(amp_b, virt_cols, occ_rows, occ_t, kernel)
        parts = lax.all_to_all(part.reshape(split), BOTH, 0, 0, tiled=True)
        exchange = jnp.sum(parts.astype(jnp.float32), axis=0)
        amp_mine = (rhs_mine - exchange) / denom_mine
        if step < ITERS - 1:
            amp_b = sent_to_all(amp_mine.astype(jnp.bfloat16), BOTH).reshape(rhs.shape)
    return sent_to_all(amp_mine, BOTH).reshape(rhs.shape)


def solution(mesh):
    in_specs = (P("row", "col"), P(("row", "col"), None), P(("col", "row"), None), P(), P(), P())
    return jax.shard_map(body, mesh=mesh, in_specs=in_specs, out_specs=P(), check_vma=False)
```

```python
import functools

import jax
import jax.numpy as jnp
from jax import lax
from jax.experimental import pallas as pl
from jax.experimental.pallas import tpu as pltpu
from jax.sharding import PartitionSpec as P


ITERS = 2
LANES = 128
BOTH = ("row", "col")
NT = (((1,), (1,)), ((), ()))


def sent_to_all(shard, axis):
    peers = lax.axis_size(axis)
    return lax.all_to_all(
        jnp.broadcast_to(shard[None], (peers, *shard.shape)), axis, 0, 0, tiled=True
    )


def gathered_by_hops(shard, axis, masks):
    peers = lax.axis_size(axis)
    held, known = shard[None], [0]
    for mask in masks:
        other = lax.ppermute(held, axis, [(i, i ^ mask) for i in range(peers)])
        held = jnp.concatenate([held, other], 0)
        known = known + [k ^ mask for k in known]
    order = [known.index(m) for m in range(peers)]
    assert sorted(known) == list(range(peers))
    return held, order


def gathered_occ(occ):
    held, order = gathered_by_hops(occ, "col", (2, 4, 8, 1))
    mine = lax.axis_index("col")
    placed = pl.pallas_call(
        functools.partial(placed_kernel, order),
        out_shape=jax.ShapeDtypeStruct(held.shape, held.dtype),
        in_specs=[
            pl.BlockSpec(memory_space=pltpu.SMEM),
            pl.BlockSpec(memory_space=pltpu.VMEM),
        ],
        out_specs=pl.BlockSpec(memory_space=pltpu.VMEM),
        compiler_params=pltpu.CompilerParams(vmem_limit_bytes=4 << 20),
    )(mine.reshape(1), held)
    return placed.reshape(-1, occ.shape[1])


def placed_kernel(order, mine_ref, held_ref, out_ref):
    mine = mine_ref[0]
    for m, k in enumerate(order):
        out_ref[jnp.bitwise_xor(mine, m)] = held_ref[k]


def response_kernel(wide, amp_ref, virt_ref, occ_ref, occ_t_ref, kern_ref, out_ref, held_ref, sem):
    f32, b16 = jnp.float32, jnp.bfloat16
    chunks = kern_ref.shape[1] // wide
    copies = [
        pltpu.make_async_copy(
            kern_ref.at[:, pl.ds(chunk * wide, wide)], held_ref.at[chunk], sem.at[chunk]
        )
        for chunk in range(chunks)
    ]
    for copy in copies:
        copy.start()
    total = None
    for chunk, copy in enumerate(copies):
        virt = virt_ref[pl.ds(chunk * wide, wide), :]
        w = lax.dot_general(amp_ref[...], virt, NT, preferred_element_type=f32).astype(b16)
        outer = jnp.dot(occ_ref[...], w, preferred_element_type=f32)
        copy.wait()
        weighted = (held_ref[chunk].astype(f32) * outer).astype(b16)
        contracted = jnp.dot(occ_t_ref[...], weighted, preferred_element_type=f32)
        high = contracted.astype(b16)
        low = (contracted - high.astype(f32)).astype(b16)
        exchange = jnp.dot(high, virt, preferred_element_type=f32)
        exchange += jnp.dot(low, virt, preferred_element_type=f32)
        total = exchange if total is None else total + exchange
    out_ref[...] = total.astype(out_ref.dtype)


def partial_exchange(amp_b, virt_cols, occ_rows, occ_t, kernel):
    rows, cols = kernel.shape
    wide = 256
    vmem = pl.BlockSpec(memory_space=pltpu.VMEM)
    return pl.pallas_call(
        functools.partial(response_kernel, wide),
        out_shape=jax.ShapeDtypeStruct(amp_b.shape, jnp.bfloat16),
        in_specs=[vmem, vmem, vmem, vmem, pl.BlockSpec(memory_space=pltpu.HBM)],
        out_specs=vmem,
        scratch_shapes=[
            pltpu.VMEM((cols // wide, rows, wide), jnp.bfloat16),
            pltpu.SemaphoreType.DMA((cols // wide,)),
        ],
        compiler_params=pltpu.CompilerParams(vmem_limit_bytes=40 << 20),
    )(amp_b, virt_cols, occ_rows, occ_t, pltpu.with_memory_space_constraint(kernel, pltpu.HBM))


def body(kernel, occ, virt, rhs, e_occ, e_virt):
    occupied, virtual = rhs.shape
    split = (occupied, virtual // LANES, LANES)
    mine = lax.axis_index("row") * lax.axis_size("col") + lax.axis_index("col")
    virt_cols = sent_to_all(virt, "row").reshape(-1, virtual)
    occ_rows = gathered_occ(occ)
    occ_t = occ_rows.T
    rhs_mine = lax.dynamic_index_in_dim(rhs, mine, 0, False).reshape(split[1:])
    denom_mine = e_virt.reshape(split[1:]) - lax.dynamic_index_in_dim(e_occ, mine, 0, False)

    amp_b = (rhs / (e_virt[None, :] - e_occ[:, None])).astype(jnp.bfloat16)
    for step in range(ITERS):
        part = partial_exchange(amp_b, virt_cols, occ_rows, occ_t, kernel)
        parts = lax.all_to_all(part.reshape(split), BOTH, 0, 0, tiled=True)
        exchange = jnp.sum(parts.astype(jnp.float32), axis=0)
        amp_mine = (rhs_mine - exchange) / denom_mine
        if step < ITERS - 1:
            amp_b = sent_to_all(amp_mine.astype(jnp.bfloat16), BOTH).reshape(rhs.shape)
    return sent_to_all(amp_mine, BOTH).reshape(rhs.shape)


def solution(mesh):
    in_specs = (P("row", "col"), P(("row", "col"), None), P(("col", "row"), None), P(), P(), P())
    return jax.shard_map(body, mesh=mesh, in_specs=in_specs, out_specs=P(), check_vma=False)
```

```python
import functools

import jax
import jax.numpy as jnp
from jax import lax
from jax.experimental import pallas as pl
from jax.experimental.pallas import tpu as pltpu
from jax.sharding import PartitionSpec as P


ITERS = 2
LANES = 128
BOTH = ("row", "col")
NT = (((1,), (1,)), ((), ()))
TN = (((0,), (0,)), ((), ()))
VMEM = pl.BlockSpec(memory_space=pltpu.VMEM)
SMEM = pl.BlockSpec(memory_space=pltpu.SMEM)
HBM = pl.BlockSpec(memory_space=pltpu.HBM)


def sent_to_all(shard, axis):
    peers = lax.axis_size(axis)
    return lax.all_to_all(
        jnp.broadcast_to(shard[None], (peers, *shard.shape)), axis, 0, 0, tiled=True
    )


def place_kernel(axis, order, held_ref, out_ref):
    mine, tall = lax.axis_index(axis), held_ref.shape[1]
    for m, k in enumerate(order):
        start = pl.multiple_of(jnp.bitwise_xor(mine, m) * tall, tall)
        out_ref[pl.ds(start, tall), :] = held_ref[k]


def gathered_by_hops(shard, axis, masks):
    peers = lax.axis_size(axis)
    held, known = shard[None], [0]
    for mask in masks:
        other = lax.ppermute(held, axis, [(i, i ^ mask) for i in range(peers)])
        held = jnp.concatenate([held, other], 0)
        known = known + [k ^ mask for k in known]
    order = [known.index(m) for m in range(peers)]
    return pl.pallas_call(
        functools.partial(place_kernel, axis, order),
        out_shape=jax.ShapeDtypeStruct((peers * shard.shape[0], shard.shape[1]), shard.dtype),
        in_specs=[VMEM],
        out_specs=VMEM,
        compiler_params=pltpu.CompilerParams(vmem_limit_bytes=4 << 20),
    )(held)


def own_kernel(e_occ_ref, rhs_ref, e_virt_ref, rhs_mine_ref, denom_ref):
    tall, lanes = denom_ref.shape
    mine = lax.axis_index("row") * lax.axis_size("col") + lax.axis_index("col")
    group, part = mine // e_virt_ref.shape[0], mine % e_virt_ref.shape[0]
    pair = rhs_ref[
        pl.ds(pl.multiple_of(group // 2 * (2 * tall), 2 * tall), 2 * tall),
        pl.ds(pl.multiple_of(part * lanes, lanes), lanes),
    ]
    rhs_mine_ref[...] = jnp.where(group % 2 == 0, pair[:tall], pair[tall:])
    for row in range(tall):
        denom_ref[pl.ds(row, 1), :] = e_virt_ref[pl.ds(part, 1), :] - e_occ_ref[group * tall + row]


def own_block(rhs, e_occ, e_virt, tall):
    small = jax.ShapeDtypeStruct((tall, LANES), jnp.float32)
    return pl.pallas_call(
        own_kernel,
        out_shape=(small, small),
        in_specs=[SMEM, VMEM, VMEM],
        out_specs=(VMEM, VMEM),
        compiler_params=pltpu.CompilerParams(vmem_limit_bytes=1 << 20),
    )(e_occ, rhs, e_virt.reshape(-1, LANES))


def put_together(blocks_ref, out_ref):
    count, tall, lanes = blocks_ref.shape
    parts = out_ref.shape[1] // lanes
    for block in range(count):
        row, column = block // parts * tall, block % parts * lanes
        out_ref[row : row + tall, column : column + lanes] = blocks_ref[block]


def whole(blocks, shape):
    return pl.pallas_call(
        put_together,
        out_shape=jax.ShapeDtypeStruct(shape, blocks.dtype),
        in_specs=[VMEM],
        compiler_params=pltpu.CompilerParams(vmem_limit_bytes=4 << 20),
    )(blocks)


def response_kernel(cuts, tall, amp_ref, virt_ref, occ_ref, kern_ref, out_ref, *held):
    f32, b16 = jnp.float32, jnp.bfloat16
    if len(amp_ref.shape) == 3:
        *held, joined_ref = held
        put_together(amp_ref, joined_ref)
        amp_ref = joined_ref
    blocks = occ_ref.shape[0] // tall
    waits = {}
    if cuts:
        held_ref, sem = held
        for i, (first, last) in enumerate(zip(cuts, (*cuts[1:], blocks))):
            part = pl.ds(first * tall, (last - first) * tall)
            waits[first] = pltpu.make_async_copy(kern_ref.at[part], held_ref.at[part], sem.at[i])
            waits[first].start()
        kern_ref = held_ref
    w = lax.dot_general(amp_ref[...], virt_ref[...], NT, preferred_element_type=f32).astype(b16)

    def outer_of(block):
        return jnp.dot(occ_ref[pl.ds(block * tall, tall), :], w, preferred_element_type=f32)

    ahead, contracted = outer_of(0), None
    for block in range(blocks):
        here = pl.ds(block * tall, tall)
        if block in waits:
            waits[block].wait()
        outer = ahead
        if block + 1 < blocks:
            ahead = outer_of(block + 1)
        weighted = (kern_ref[here, :].astype(f32) * outer).astype(b16)
        more = lax.dot_general(occ_ref[here, :], weighted, TN, preferred_element_type=f32)
        contracted = more if contracted is None else contracted + more
    high = contracted.astype(b16)
    low = (contracted - high.astype(f32)).astype(b16)
    exchange = jnp.dot(high, virt_ref[...], preferred_element_type=f32)
    exchange += jnp.dot(low, virt_ref[...], preferred_element_type=f32)
    _, rows, lanes = out_ref.shape
    parts = exchange.shape[1] // lanes
    for group in range(exchange.shape[0] // rows):
        for part in range(parts):
            out_ref[group * parts + part] = exchange[
                group * rows : (group + 1) * rows, part * lanes : (part + 1) * lanes
            ].astype(out_ref.dtype)


def partial_exchange(amp_b, virt_cols, occ_rows, kernel, pieces, cuts=()):
    out = jax.ShapeDtypeStruct(pieces, jnp.bfloat16)
    held = jax.ShapeDtypeStruct(kernel.shape, kernel.dtype)
    return pl.pallas_call(
        functools.partial(response_kernel, cuts, 512),
        out_shape=(out, held) if cuts else out,
        in_specs=[VMEM, VMEM, VMEM, HBM if cuts else VMEM],
        out_specs=(VMEM, VMEM) if cuts else VMEM,
        scratch_shapes=[pltpu.SemaphoreType.DMA((len(cuts),))]
        if cuts
        else [pltpu.VMEM((occ_rows.shape[1], virt_cols.shape[1]), jnp.bfloat16)],
        compiler_params=pltpu.CompilerParams(vmem_limit_bytes=40 << 20),
    )(amp_b, virt_cols, occ_rows, kernel)


def body(kernel, occ, virt, rhs, e_occ, e_virt):
    occupied, virtual = rhs.shape
    devices = lax.axis_size(BOTH)
    pieces = (devices, occupied * virtual // (devices * LANES), LANES)
    virt_cols = sent_to_all(virt, "row").reshape(-1, virtual)
    occ_rows = gathered_by_hops(occ, "col", (8, 4, 2, 1))
    rhs_mine, denom_mine = own_block(rhs, e_occ, e_virt, pieces[1])

    amp_b = (rhs / (e_virt[None, :] - e_occ[:, None])).astype(jnp.bfloat16)
    kernel = pltpu.with_memory_space_constraint(kernel, pltpu.HBM)
    for step in range(ITERS):
        if step == 0:
            part, kernel = partial_exchange(amp_b, virt_cols, occ_rows, kernel, pieces, (0, 2))
        else:
            part = partial_exchange(amp_b, virt_cols, occ_rows, kernel, pieces)
        parts = lax.all_to_all(part, BOTH, 0, 0, tiled=True)
        exchange = jnp.sum(parts.astype(jnp.float32), axis=0)
        amp_mine = (rhs_mine - exchange) / denom_mine
        if step < ITERS - 1:
            amp_b = sent_to_all(amp_mine.astype(jnp.bfloat16), BOTH)
    return whole(sent_to_all(amp_mine, BOTH), rhs.shape)


def solution(mesh):
    in_specs = (P("row", "col"), P(("row", "col"), None), P(("col", "row"), None), P(), P(), P())
    return jax.shard_map(body, mesh=mesh, in_specs=in_specs, out_specs=P(), check_vma=False)
```

```python
import functools

import jax
import jax.numpy as jnp
from jax import lax
from jax.experimental import pallas as pl
from jax.experimental.pallas import tpu as pltpu
from jax.sharding import PartitionSpec as P


ITERS = 2
LANES = 128
BOTH = ("row", "col")
NT = (((1,), (1,)), ((), ()))
TN = (((0,), (0,)), ((), ()))
VMEM = pl.BlockSpec(memory_space=pltpu.VMEM)
SMEM = pl.BlockSpec(memory_space=pltpu.SMEM)
HBM = pl.BlockSpec(memory_space=pltpu.HBM)


def sent_to_all(shard, axis):
    peers = lax.axis_size(axis)
    return lax.all_to_all(
        jnp.broadcast_to(shard[None], (peers, *shard.shape)), axis, 0, 0, tiled=True
    )


def place_kernel(axis, order, held_ref, out_ref):
    mine, tall = lax.axis_index(axis), held_ref.shape[1]
    for m, k in enumerate(order):
        start = pl.multiple_of(jnp.bitwise_xor(mine, m) * tall, tall)
        out_ref[pl.ds(start, tall), :] = held_ref[k]


def gathered_by_hops(source, shard, axis, masks):
    peers = lax.axis_size(axis)
    held, known = shard[None], [0]
    for stage, mask in enumerate(masks):
        sent = held if stage else source[None]
        other = lax.ppermute(sent, axis, [(i, i ^ mask) for i in range(peers)])
        held = jnp.concatenate([held, other], 0)
        known = known + [k ^ mask for k in known]
    order = [known.index(m) for m in range(peers)]
    return pl.pallas_call(
        functools.partial(place_kernel, axis, order),
        out_shape=jax.ShapeDtypeStruct((peers * shard.shape[0], shard.shape[1]), shard.dtype),
        in_specs=[VMEM],
        out_specs=VMEM,
        compiler_params=pltpu.CompilerParams(vmem_limit_bytes=4 << 20),
    )(held)


def stage_kernel(
    virt_ref, occ_ref, rhs_ref, e_occ_ref, e_virt_ref,
    copies_ref, occ_out_ref, amp_ref, rhs_mine_ref, denom_mine_ref,
    virt_here, rhs_here, e_occ_here, e_virt_here, denom_here, sem_in, sem_out,
):
    pairs = (
        (virt_ref, virt_here),
        (rhs_ref, rhs_here),
        (e_occ_ref, e_occ_here),
        (e_virt_ref, e_virt_here),
        (occ_ref, occ_out_ref),
    )
    fetches = [pltpu.make_async_copy(*pair, sem_in.at[i]) for i, pair in enumerate(pairs)]
    for fetch in fetches:
        fetch.start()
    fetches[0].wait()
    sends = [
        pltpu.make_async_copy(virt_here, copies_ref.at[peer], sem_out.at[peer])
        for peer in range(copies_ref.shape[0])
    ]
    for send in sends:
        send.start()
    for fetch in fetches[1:]:
        fetch.wait()
    denom = e_virt_here[...] - e_occ_here[...].T
    denom_here[...] = denom
    amp_ref[...] = (rhs_here[...] / denom).astype(amp_ref.dtype)
    tall, lanes = denom_mine_ref.shape
    parts = rhs_here.shape[1] // lanes
    mine = lax.axis_index("row") * lax.axis_size("col") + lax.axis_index("col")
    group, part = mine // parts, mine % parts
    rows = pl.ds(pl.multiple_of(group // 2 * (2 * tall), 2 * tall), 2 * tall)
    columns = pl.ds(pl.multiple_of(part * lanes, lanes), lanes)
    for from_ref, to_ref in ((rhs_here, rhs_mine_ref), (denom_here, denom_mine_ref)):
        pair = from_ref[rows, columns]
        to_ref[...] = jnp.where(group % 2 == 0, pair[:tall], pair[tall:])
    for send in sends:
        send.wait()


def staged(virt, occ, rhs, e_occ, e_virt, tall):
    f32, b16 = jnp.float32, jnp.bfloat16
    peers = lax.axis_size("row")
    small = jax.ShapeDtypeStruct((tall, LANES), f32)
    args = [
        pltpu.with_memory_space_constraint(array, pltpu.HBM)
        for array in (virt, occ, rhs, e_occ.reshape(1, -1), e_virt.reshape(1, -1))
    ]
    return pl.pallas_call(
        stage_kernel,
        out_shape=(
            jax.ShapeDtypeStruct((peers, *virt.shape), b16),
            jax.ShapeDtypeStruct(occ.shape, b16),
            jax.ShapeDtypeStruct(rhs.shape, b16),
            small,
            small,
        ),
        in_specs=[HBM] * 5,
        out_specs=(HBM, VMEM, VMEM, VMEM, VMEM),
        scratch_shapes=[
            pltpu.VMEM(virt.shape, b16),
            pltpu.VMEM(rhs.shape, f32),
            pltpu.VMEM((1, rhs.shape[0]), f32),
            pltpu.VMEM((1, rhs.shape[1]), f32),
            pltpu.VMEM(rhs.shape, f32),
            pltpu.SemaphoreType.DMA((5,)),
            pltpu.SemaphoreType.DMA((peers,)),
        ],
        compiler_params=pltpu.CompilerParams(vmem_limit_bytes=4 << 20),
    )(*args)


def put_together(blocks_ref, out_ref):
    count, tall, lanes = blocks_ref.shape
    parts = out_ref.shape[1] // lanes
    for block in range(count):
        row, column = block // parts * tall, block % parts * lanes
        out_ref[row : row + tall, column : column + lanes] = blocks_ref[block]


def whole(blocks, shape):
    return pl.pallas_call(
        put_together,
        out_shape=jax.ShapeDtypeStruct(shape, blocks.dtype),
        in_specs=[VMEM],
        compiler_params=pltpu.CompilerParams(vmem_limit_bytes=4 << 20),
    )(blocks)


def response_kernel(cuts, tall, amp_ref, virt_ref, occ_ref, kern_ref, out_ref, *held):
    f32, b16 = jnp.float32, jnp.bfloat16
    if len(amp_ref.shape) == 3:
        *held, joined_ref = held
        put_together(amp_ref, joined_ref)
        amp_ref = joined_ref
    blocks = occ_ref.shape[0] // tall
    waits = {}
    if cuts:
        held_ref, sem = held
        for i, (first, last) in enumerate(zip(cuts, (*cuts[1:], blocks))):
            part = pl.ds(first * tall, (last - first) * tall)
            waits[first] = pltpu.make_async_copy(kern_ref.at[part], held_ref.at[part], sem.at[i])
            waits[first].start()
        kern_ref = held_ref
    w = lax.dot_general(amp_ref[...], virt_ref[...], NT, preferred_element_type=f32).astype(b16)

    def outer_of(block):
        return jnp.dot(occ_ref[pl.ds(block * tall, tall), :], w, preferred_element_type=f32)

    ahead, contracted = outer_of(0), None
    for block in range(blocks):
        here = pl.ds(block * tall, tall)
        if block in waits:
            waits[block].wait()
        outer = ahead
        if block + 1 < blocks:
            ahead = outer_of(block + 1)
        weighted = (kern_ref[here, :].astype(f32) * outer).astype(b16)
        more = lax.dot_general(occ_ref[here, :], weighted, TN, preferred_element_type=f32)
        contracted = more if contracted is None else contracted + more
    high = contracted.astype(b16)
    low = (contracted - high.astype(f32)).astype(b16)
    exchange = jnp.dot(high, virt_ref[...], preferred_element_type=f32)
    exchange += jnp.dot(low, virt_ref[...], preferred_element_type=f32)
    _, rows, lanes = out_ref.shape
    parts = exchange.shape[1] // lanes
    for group in range(exchange.shape[0] // rows):
        for part in range(parts):
            out_ref[group * parts + part] = exchange[
                group * rows : (group + 1) * rows, part * lanes : (part + 1) * lanes
            ].astype(out_ref.dtype)


def partial_exchange(amp_b, virt_cols, occ_rows, kernel, pieces, cuts=()):
    out = jax.ShapeDtypeStruct(pieces, jnp.bfloat16)
    held = jax.ShapeDtypeStruct(kernel.shape, kernel.dtype)
    return pl.pallas_call(
        functools.partial(response_kernel, cuts, 512),
        out_shape=(out, held) if cuts else out,
        in_specs=[VMEM, VMEM, VMEM, HBM if cuts else VMEM],
        out_specs=(VMEM, VMEM) if cuts else VMEM,
        scratch_shapes=[pltpu.SemaphoreType.DMA((len(cuts),))]
        if cuts
        else [pltpu.VMEM((occ_rows.shape[1], virt_cols.shape[1]), jnp.bfloat16)],
        compiler_params=pltpu.CompilerParams(vmem_limit_bytes=40 << 20),
    )(amp_b, virt_cols, occ_rows, kernel)


def body(kernel, occ, virt, rhs, e_occ, e_virt):
    occupied, virtual = rhs.shape
    devices = lax.axis_size(BOTH)
    pieces = (devices, occupied * virtual // (devices * LANES), LANES)
    copies, occ_here, amp_b, rhs_mine, denom_mine = staged(virt, occ, rhs, e_occ, e_virt, pieces[1])
    virt_cols = lax.all_to_all(copies, "row", 0, 0, tiled=True).reshape(-1, virtual)
    occ_rows = gathered_by_hops(occ, occ_here, "col", (8, 4, 2, 1))

    kernel = pltpu.with_memory_space_constraint(kernel, pltpu.HBM)
    for step in range(ITERS):
        if step == 0:
            part, kernel = partial_exchange(amp_b, virt_cols, occ_rows, kernel, pieces, (0, 2))
        else:
            part = partial_exchange(amp_b, virt_cols, occ_rows, kernel, pieces)
        parts = lax.all_to_all(part, BOTH, 0, 0, tiled=True)
        exchange = jnp.sum(parts.astype(jnp.float32), axis=0)
        amp_mine = (rhs_mine - exchange) / denom_mine
        if step < ITERS - 1:
            amp_b = sent_to_all(amp_mine.astype(jnp.bfloat16), BOTH)
    return whole(sent_to_all(amp_mine, BOTH), rhs.shape)


def solution(mesh):
    in_specs = (P("row", "col"), P(("row", "col"), None), P(("col", "row"), None), P(), P(), P())
    return jax.shard_map(body, mesh=mesh, in_specs=in_specs, out_specs=P(), check_vma=False)
```

```python
import functools

import jax
import jax.numpy as jnp
from jax import lax
from jax.experimental import pallas as pl
from jax.experimental.pallas import tpu as pltpu
from jax.sharding import PartitionSpec as P


ITERS = 2
LANES = 128
BOTH = ("row", "col")
SEQUENCE = (2, 4, 3, 7, 6, 1, 0, 5)
NT = (((1,), (1,)), ((), ()))
TN = (((0,), (0,)), ((), ()))
VMEM = pl.BlockSpec(memory_space=pltpu.VMEM)
SMEM = pl.BlockSpec(memory_space=pltpu.SMEM)
HBM = pl.BlockSpec(memory_space=pltpu.HBM)


def sent_to_all(shard, axis):
    peers = lax.axis_size(axis)
    return lax.all_to_all(
        jnp.broadcast_to(shard[None], (peers, *shard.shape)), axis, 0, 0, tiled=True
    )


def place_kernel(axis, order, held_ref, out_ref):
    mine, tall = lax.axis_index(axis), held_ref.shape[1]
    for m, k in enumerate(order):
        start = pl.multiple_of(jnp.bitwise_xor(mine, m) * tall, tall)
        out_ref[pl.ds(start, tall), :] = held_ref[k]


def gathered_by_hops(source, shard, axis, masks):
    peers = lax.axis_size(axis)
    held, known = shard[None], [0]
    for stage, mask in enumerate(masks):
        sent = held if stage else source[None]
        other = lax.ppermute(sent, axis, [(i, i ^ mask) for i in range(peers)])
        held = jnp.concatenate([held, other], 0)
        known = known + [k ^ mask for k in known]
    order = [known.index(m) for m in range(peers)]
    return pl.pallas_call(
        functools.partial(place_kernel, axis, order),
        out_shape=jax.ShapeDtypeStruct((peers * shard.shape[0], shard.shape[1]), shard.dtype),
        in_specs=[VMEM],
        out_specs=VMEM,
        compiler_params=pltpu.CompilerParams(vmem_limit_bytes=4 << 20),
    )(held)


def gathered_by_rows(copies):
    cols = lax.axis_size("col")
    groups = [[row * cols + col for row in SEQUENCE] for col in range(cols)]
    return lax.all_to_all(copies, BOTH, 0, 0, tiled=True, axis_index_groups=groups)


def stage_kernel(
    virt_ref, occ_ref, rhs_ref, e_occ_ref, e_virt_ref,
    copies_ref, occ_out_ref, amp_ref, rhs_mine_ref, denom_mine_ref,
    virt_here, rhs_here, e_occ_here, e_virt_here, denom_here, sem_in, sem_out,
):
    pairs = (
        (virt_ref, virt_here),
        (rhs_ref, rhs_here),
        (e_occ_ref, e_occ_here),
        (e_virt_ref, e_virt_here),
        (occ_ref, occ_out_ref),
    )
    fetches = [pltpu.make_async_copy(*pair, sem_in.at[i]) for i, pair in enumerate(pairs)]
    for fetch in fetches:
        fetch.start()
    fetches[0].wait()
    sends = [
        pltpu.make_async_copy(virt_here, copies_ref.at[peer], sem_out.at[peer])
        for peer in range(copies_ref.shape[0])
    ]
    for send in sends:
        send.start()
    for fetch in fetches[1:]:
        fetch.wait()
    denom = e_virt_here[...] - e_occ_here[...].T
    denom_here[...] = denom
    amp_ref[...] = (rhs_here[...] / denom).astype(amp_ref.dtype)
    tall, lanes = denom_mine_ref.shape
    parts = rhs_here.shape[1] // lanes
    mine = lax.axis_index("row") * lax.axis_size("col") + lax.axis_index("col")
    group, part = mine // parts, mine % parts
    rows = pl.ds(pl.multiple_of(group // 2 * (2 * tall), 2 * tall), 2 * tall)
    columns = pl.ds(pl.multiple_of(part * lanes, lanes), lanes)
    for from_ref, to_ref in ((rhs_here, rhs_mine_ref), (denom_here, denom_mine_ref)):
        pair = from_ref[rows, columns]
        to_ref[...] = jnp.where(group % 2 == 0, pair[:tall], pair[tall:])
    for send in sends:
        send.wait()


def staged(virt, occ, rhs, e_occ, e_virt, tall):
    f32, b16 = jnp.float32, jnp.bfloat16
    peers = lax.axis_size("row")
    small = jax.ShapeDtypeStruct((tall, LANES), f32)
    args = [
        pltpu.with_memory_space_constraint(array, pltpu.HBM)
        for array in (virt, occ, rhs, e_occ.reshape(1, -1), e_virt.reshape(1, -1))
    ]
    return pl.pallas_call(
        stage_kernel,
        out_shape=(
            jax.ShapeDtypeStruct((peers, *virt.shape), b16),
            jax.ShapeDtypeStruct(occ.shape, b16),
            jax.ShapeDtypeStruct(rhs.shape, b16),
            small,
            small,
        ),
        in_specs=[HBM] * 5,
        out_specs=(HBM, VMEM, VMEM, VMEM, VMEM),
        scratch_shapes=[
            pltpu.VMEM(virt.shape, b16),
            pltpu.VMEM(rhs.shape, f32),
            pltpu.VMEM((1, rhs.shape[0]), f32),
            pltpu.VMEM((1, rhs.shape[1]), f32),
            pltpu.VMEM(rhs.shape, f32),
            pltpu.SemaphoreType.DMA((5,)),
            pltpu.SemaphoreType.DMA((peers,)),
        ],
        compiler_params=pltpu.CompilerParams(vmem_limit_bytes=4 << 20),
    )(*args)


def put_together(blocks_ref, out_ref):
    count, tall, lanes = blocks_ref.shape
    parts = out_ref.shape[1] // lanes
    for block in range(count):
        row, column = block // parts * tall, block % parts * lanes
        out_ref[row : row + tall, column : column + lanes] = blocks_ref[block].astype(out_ref.dtype)


def last_kernel(blocks_ref, rhs_ref, e_occ_ref, e_virt_ref, out_ref, exchange_ref):
    put_together(blocks_ref, exchange_ref)
    denom = e_virt_ref[...] - e_occ_ref[...].T
    out_ref[...] = (rhs_ref[...] - exchange_ref[...]) / denom


def last_amplitudes(blocks, rhs, e_occ, e_virt):
    return pl.pallas_call(
        last_kernel,
        out_shape=jax.ShapeDtypeStruct(rhs.shape, jnp.float32),
        in_specs=[VMEM] * 4,
        scratch_shapes=[pltpu.VMEM(rhs.shape, jnp.float32)],
        compiler_params=pltpu.CompilerParams(vmem_limit_bytes=4 << 20),
    )(blocks, rhs, e_occ.reshape(1, -1), e_virt.reshape(1, -1))


def response_kernel(cuts, tall, amp_ref, virt_ref, occ_ref, kern_ref, out_ref, *held):
    f32, b16 = jnp.float32, jnp.bfloat16
    blocks = occ_ref.shape[0] // tall
    waits = {}
    if cuts:
        held_ref, ordered_ref, sem = held
        for i, (first, last) in enumerate(zip(cuts, (*cuts[1:], blocks))):
            part = pl.ds(first * tall, (last - first) * tall)
            waits[first] = pltpu.make_async_copy(kern_ref.at[part], held_ref.at[part], sem.at[i])
            waits[first].start()
        share = virt_ref.shape[1]
        for i, row in enumerate(SEQUENCE):
            ordered_ref[row * share : (row + 1) * share, :] = virt_ref[i]
        kern_ref, virt_ref = held_ref, ordered_ref
    else:
        (joined_ref,) = held
        put_together(amp_ref, joined_ref)
        amp_ref = joined_ref
    w = lax.dot_general(amp_ref[...], virt_ref[...], NT, preferred_element_type=f32).astype(b16)

    def outer_of(block):
        return jnp.dot(occ_ref[pl.ds(block * tall, tall), :], w, preferred_element_type=f32)

    ahead, contracted = outer_of(0), None
    for block in range(blocks):
        here = pl.ds(block * tall, tall)
        if block in waits:
            waits[block].wait()
        outer = ahead
        if block + 1 < blocks:
            ahead = outer_of(block + 1)
        weighted = (kern_ref[here, :].astype(f32) * outer).astype(b16)
        more = lax.dot_general(occ_ref[here, :], weighted, TN, preferred_element_type=f32)
        contracted = more if contracted is None else contracted + more
    high = contracted.astype(b16)
    low = (contracted - high.astype(f32)).astype(b16)
    exchange = jnp.dot(high, virt_ref[...], preferred_element_type=f32)
    exchange += jnp.dot(low, virt_ref[...], preferred_element_type=f32)
    _, rows, lanes = out_ref.shape
    parts = exchange.shape[1] // lanes
    for group in range(exchange.shape[0] // rows):
        for part in range(parts):
            out_ref[group * parts + part] = exchange[
                group * rows : (group + 1) * rows, part * lanes : (part + 1) * lanes
            ].astype(out_ref.dtype)


def first_exchange(amp_b, virt_blocks, occ_rows, kernel, pieces):
    peers, share, virtual = virt_blocks.shape
    cuts, b16 = (0, 2), jnp.bfloat16
    return pl.pallas_call(
        functools.partial(response_kernel, cuts, 512),
        out_shape=(
            jax.ShapeDtypeStruct(pieces, b16),
            jax.ShapeDtypeStruct(kernel.shape, b16),
            jax.ShapeDtypeStruct((peers * share, virtual), b16),
        ),
        in_specs=[VMEM, VMEM, VMEM, HBM],
        out_specs=(VMEM, VMEM, VMEM),
        scratch_shapes=[pltpu.SemaphoreType.DMA((len(cuts),))],
        compiler_params=pltpu.CompilerParams(vmem_limit_bytes=40 << 20),
    )(amp_b, virt_blocks, occ_rows, pltpu.with_memory_space_constraint(kernel, pltpu.HBM))


def next_exchange(amp_blocks, virt_cols, occ_rows, kernel):
    return pl.pallas_call(
        functools.partial(response_kernel, (), 512),
        out_shape=jax.ShapeDtypeStruct(amp_blocks.shape, jnp.bfloat16),
        in_specs=[VMEM] * 4,
        out_specs=VMEM,
        scratch_shapes=[pltpu.VMEM((occ_rows.shape[1], virt_cols.shape[1]), jnp.bfloat16)],
        compiler_params=pltpu.CompilerParams(vmem_limit_bytes=40 << 20),
    )(amp_blocks, virt_cols, occ_rows, kernel)


def body(kernel, occ, virt, rhs, e_occ, e_virt):
    occupied, virtual = rhs.shape
    devices = lax.axis_size(BOTH)
    pieces = (devices, occupied * virtual // (devices * LANES), LANES)
    copies, occ_here, amp_b, rhs_mine, denom_mine = staged(
        virt, occ, rhs, e_occ, e_virt, pieces[1]
    )
    virt_blocks = gathered_by_rows(copies)
    occ_rows = gathered_by_hops(occ, occ_here, "col", (8, 4, 2, 1))

    for step in range(ITERS):
        if step == 0:
            part, kernel, virt_cols = first_exchange(amp_b, virt_blocks, occ_rows, kernel, pieces)
        else:
            part = next_exchange(amp_b, virt_cols, occ_rows, kernel)
        parts = lax.all_to_all(part, BOTH, 0, 0, tiled=True)
        exchange = jnp.sum(parts.astype(jnp.float32), axis=0)
        if step < ITERS - 1:
            amp_mine = (rhs_mine - exchange) / denom_mine
            amp_b = sent_to_all(amp_mine.astype(jnp.bfloat16), BOTH)
    return last_amplitudes(sent_to_all(exchange.astype(jnp.bfloat16), BOTH), rhs, e_occ, e_virt)


def solution(mesh):
    in_specs = (P("row", "col"), P(("row", "col"), None), P(("col", "row"), None), P(), P(), P())
    return jax.shard_map(body, mesh=mesh, in_specs=in_specs, out_specs=P(), check_vma=False)
```

```python
import functools

import jax
import jax.numpy as jnp
from jax import lax
from jax.experimental import pallas as pl
from jax.experimental.pallas import tpu as pltpu
from jax.sharding import PartitionSpec as P


ITERS = 2
LANES = 128
TALL = 512
BOTH = ("row", "col")
SEQUENCE = (3, 5, 2, 6, 7, 0, 1, 4)
NT = (((1,), (1,)), ((), ()))
TN = (((0,), (0,)), ((), ()))
VMEM = pl.BlockSpec(memory_space=pltpu.VMEM)
SMEM = pl.BlockSpec(memory_space=pltpu.SMEM)
HBM = pl.BlockSpec(memory_space=pltpu.HBM)


def sent_to_all(shard, axis):
    peers = lax.axis_size(axis)
    return lax.all_to_all(
        jnp.broadcast_to(shard[None], (peers, *shard.shape)), axis, 0, 0, tiled=True
    )


def place_kernel(axis, order, held_ref, out_ref):
    mine, tall = lax.axis_index(axis), held_ref.shape[1]
    for m, k in enumerate(order):
        start = pl.multiple_of(jnp.bitwise_xor(mine, m) * tall, tall)
        out_ref[pl.ds(start, tall), :] = held_ref[k]


def gathered_by_hops(source, shard, axis, masks):
    peers = lax.axis_size(axis)
    held, known = shard[None], [0]
    for stage, mask in enumerate(masks):
        sent = held if stage else source[None]
        other = lax.ppermute(sent, axis, [(i, i ^ mask) for i in range(peers)])
        held = jnp.concatenate([held, other], 0)
        known = known + [k ^ mask for k in known]
    order = [known.index(m) for m in range(peers)]
    return pl.pallas_call(
        functools.partial(place_kernel, axis, order),
        out_shape=jax.ShapeDtypeStruct((peers * shard.shape[0], shard.shape[1]), shard.dtype),
        in_specs=[VMEM],
        out_specs=VMEM,
        compiler_params=pltpu.CompilerParams(vmem_limit_bytes=4 << 20),
    )(held)


def gathered_by_rows(copies):
    cols = lax.axis_size("col")
    groups = [[row * cols + col for row in SEQUENCE] for col in range(cols)]
    return lax.all_to_all(copies, BOTH, 0, 0, tiled=True, axis_index_groups=groups)


def stage_kernel(
    virt_ref, occ_ref, rhs_ref, e_occ_ref, e_virt_ref,
    copies_ref, occ_out_ref, amp_ref, rhs_mine_ref, denom_mine_ref,
    virt_here, rhs_here, e_occ_here, e_virt_here, denom_here, sem_in, sem_out,
):
    pairs = (
        (virt_ref, virt_here),
        (rhs_ref, rhs_here),
        (e_occ_ref, e_occ_here),
        (e_virt_ref, e_virt_here),
        (occ_ref, occ_out_ref),
    )
    fetches = [pltpu.make_async_copy(*pair, sem_in.at[i]) for i, pair in enumerate(pairs)]
    for fetch in fetches:
        fetch.start()
    fetches[0].wait()
    sends = [
        pltpu.make_async_copy(virt_here, copies_ref.at[peer], sem_out.at[peer])
        for peer in range(copies_ref.shape[0])
    ]
    for send in sends:
        send.start()
    for fetch in fetches[1:]:
        fetch.wait()
    denom = e_virt_here[...] - e_occ_here[...].T
    denom_here[...] = denom
    amp_ref[...] = (rhs_here[...] / denom).astype(amp_ref.dtype)
    tall, lanes = denom_mine_ref.shape
    parts = rhs_here.shape[1] // lanes
    mine = lax.axis_index("row") * lax.axis_size("col") + lax.axis_index("col")
    group, part = mine // parts, mine % parts
    rows = pl.ds(pl.multiple_of(group // 2 * (2 * tall), 2 * tall), 2 * tall)
    columns = pl.ds(pl.multiple_of(part * lanes, lanes), lanes)
    for from_ref, to_ref in ((rhs_here, rhs_mine_ref), (denom_here, denom_mine_ref)):
        pair = from_ref[rows, columns]
        to_ref[...] = jnp.where(group % 2 == 0, pair[:tall], pair[tall:])
    for send in sends:
        send.wait()


def staged(virt, occ, rhs, e_occ, e_virt, tall):
    f32, b16 = jnp.float32, jnp.bfloat16
    peers = lax.axis_size("row")
    small = jax.ShapeDtypeStruct((tall, LANES), f32)
    args = [
        pltpu.with_memory_space_constraint(array, pltpu.HBM)
        for array in (virt, occ, rhs, e_occ.reshape(1, -1), e_virt.reshape(1, -1))
    ]
    return pl.pallas_call(
        stage_kernel,
        out_shape=(
            jax.ShapeDtypeStruct((peers, *virt.shape), b16),
            jax.ShapeDtypeStruct(occ.shape, b16),
            jax.ShapeDtypeStruct(rhs.shape, b16),
            small,
            small,
        ),
        in_specs=[HBM] * 5,
        out_specs=(HBM, VMEM, VMEM, VMEM, VMEM),
        scratch_shapes=[
            pltpu.VMEM(virt.shape, b16),
            pltpu.VMEM(rhs.shape, f32),
            pltpu.VMEM((1, rhs.shape[0]), f32),
            pltpu.VMEM((1, rhs.shape[1]), f32),
            pltpu.VMEM(rhs.shape, f32),
            pltpu.SemaphoreType.DMA((5,)),
            pltpu.SemaphoreType.DMA((peers,)),
        ],
        compiler_params=pltpu.CompilerParams(vmem_limit_bytes=4 << 20),
    )(*args)


def head_kernel(kern_ref, head_ref, sem):
    copy = pltpu.make_async_copy(kern_ref.at[pl.ds(0, head_ref.shape[0])], head_ref, sem)
    copy.start()
    copy.wait()


def head_of(kernel):
    return pl.pallas_call(
        head_kernel,
        out_shape=jax.ShapeDtypeStruct((TALL, kernel.shape[1]), kernel.dtype),
        in_specs=[HBM],
        out_specs=VMEM,
        scratch_shapes=[pltpu.SemaphoreType.DMA],
        compiler_params=pltpu.CompilerParams(vmem_limit_bytes=1 << 20),
    )(pltpu.with_memory_space_constraint(kernel, pltpu.HBM))


def put_together(blocks_ref, out_ref):
    count, tall, lanes = blocks_ref.shape
    parts = out_ref.shape[1] // lanes
    for block in range(count):
        row, column = block // parts * tall, block % parts * lanes
        out_ref[row : row + tall, column : column + lanes] = blocks_ref[block].astype(out_ref.dtype)


def last_kernel(blocks_ref, rhs_ref, e_occ_ref, e_virt_ref, out_ref, exchange_ref):
    put_together(blocks_ref, exchange_ref)
    denom = e_virt_ref[...] - e_occ_ref[...].T
    out_ref[...] = (rhs_ref[...] - exchange_ref[...]) / denom


def last_amplitudes(blocks, rhs, e_occ, e_virt):
    return pl.pallas_call(
        last_kernel,
        out_shape=jax.ShapeDtypeStruct(rhs.shape, jnp.float32),
        in_specs=[VMEM] * 4,
        scratch_shapes=[pltpu.VMEM(rhs.shape, jnp.float32)],
        compiler_params=pltpu.CompilerParams(vmem_limit_bytes=4 << 20),
    )(blocks, rhs, e_occ.reshape(1, -1), e_virt.reshape(1, -1))


def response_kernel(cuts, amp_ref, virt_ref, occ_ref, head_ref, kern_ref, out_ref, *held):
    f32, b16 = jnp.float32, jnp.bfloat16
    tall = head_ref.shape[0]
    blocks = occ_ref.shape[0] // tall
    waits = {}
    if cuts:
        rest_ref, ordered_ref, sem = held
        for i, (first, last) in enumerate(zip(cuts, (*cuts[1:], blocks))):
            size = (last - first) * tall
            waits[first] = pltpu.make_async_copy(
                kern_ref.at[pl.ds(first * tall, size)],
                rest_ref.at[pl.ds((first - 1) * tall, size)],
                sem.at[i],
            )
            waits[first].start()
        share = virt_ref.shape[1]
        for i, row in enumerate(SEQUENCE):
            ordered_ref[row * share : (row + 1) * share, :] = virt_ref[i]
        kern_ref, virt_ref = rest_ref, ordered_ref
    else:
        (joined_ref,) = held
        put_together(amp_ref, joined_ref)
        amp_ref = joined_ref
    w = lax.dot_general(amp_ref[...], virt_ref[...], NT, preferred_element_type=f32).astype(b16)

    def outer_of(block):
        return jnp.dot(occ_ref[pl.ds(block * tall, tall), :], w, preferred_element_type=f32)

    ahead, contracted = outer_of(0), None
    for block in range(blocks):
        here = pl.ds(block * tall, tall)
        if block in waits:
            waits[block].wait()
        outer = ahead
        if block + 1 < blocks:
            ahead = outer_of(block + 1)
        rows_here = kern_ref[pl.ds((block - 1) * tall, tall), :] if block else head_ref[...]
        weighted = (rows_here.astype(f32) * outer).astype(b16)
        more = lax.dot_general(occ_ref[here, :], weighted, TN, preferred_element_type=f32)
        contracted = more if contracted is None else contracted + more
    high = contracted.astype(b16)
    low = (contracted - high.astype(f32)).astype(b16)
    exchange = jnp.dot(high, virt_ref[...], preferred_element_type=f32)
    exchange += jnp.dot(low, virt_ref[...], preferred_element_type=f32)
    _, rows, lanes = out_ref.shape
    parts = exchange.shape[1] // lanes
    for group in range(exchange.shape[0] // rows):
        for part in range(parts):
            out_ref[group * parts + part] = exchange[
                group * rows : (group + 1) * rows, part * lanes : (part + 1) * lanes
            ].astype(out_ref.dtype)


def first_exchange(amp_b, virt_blocks, occ_rows, head, kernel, pieces):
    peers, share, virtual = virt_blocks.shape
    cuts, b16 = (1, 3), jnp.bfloat16
    return pl.pallas_call(
        functools.partial(response_kernel, cuts),
        out_shape=(
            jax.ShapeDtypeStruct(pieces, b16),
            jax.ShapeDtypeStruct((kernel.shape[0] - head.shape[0], kernel.shape[1]), b16),
            jax.ShapeDtypeStruct((peers * share, virtual), b16),
        ),
        in_specs=[VMEM, VMEM, VMEM, VMEM, HBM],
        out_specs=(VMEM, VMEM, VMEM),
        scratch_shapes=[pltpu.SemaphoreType.DMA((len(cuts),))],
        compiler_params=pltpu.CompilerParams(vmem_limit_bytes=40 << 20),
    )(amp_b, virt_blocks, occ_rows, head, pltpu.with_memory_space_constraint(kernel, pltpu.HBM))


def next_exchange(amp_blocks, virt_cols, occ_rows, head, rest):
    return pl.pallas_call(
        functools.partial(response_kernel, ()),
        out_shape=jax.ShapeDtypeStruct(amp_blocks.shape, jnp.bfloat16),
        in_specs=[VMEM] * 5,
        out_specs=VMEM,
        scratch_shapes=[pltpu.VMEM((occ_rows.shape[1], virt_cols.shape[1]), jnp.bfloat16)],
        compiler_params=pltpu.CompilerParams(vmem_limit_bytes=40 << 20),
    )(amp_blocks, virt_cols, occ_rows, head, rest)


def body(kernel, occ, virt, rhs, e_occ, e_virt):
    occupied, virtual = rhs.shape
    devices = lax.axis_size(BOTH)
    pieces = (devices, occupied * virtual // (devices * LANES), LANES)
    copies, occ_here, amp_b, rhs_mine, denom_mine = staged(
        virt, occ, rhs, e_occ, e_virt, pieces[1]
    )
    virt_blocks = gathered_by_rows(copies)
    occ_rows = gathered_by_hops(occ, occ_here, "col", (8, 4, 2, 1))
    head = head_of(kernel)

    for step in range(ITERS):
        if step == 0:
            part, rest, virt_cols = first_exchange(
                amp_b, virt_blocks, occ_rows, head, kernel, pieces
            )
        else:
            part = next_exchange(amp_b, virt_cols, occ_rows, head, rest)
        parts = lax.all_to_all(part, BOTH, 0, 0, tiled=True)
        exchange = jnp.sum(parts.astype(jnp.float32), axis=0)
        if step < ITERS - 1:
            amp_mine = (rhs_mine - exchange) / denom_mine
            amp_b = sent_to_all(amp_mine.astype(jnp.bfloat16), BOTH)
    return last_amplitudes(sent_to_all(exchange.astype(jnp.bfloat16), BOTH), rhs, e_occ, e_virt)


def solution(mesh):
    in_specs = (P("row", "col"), P(("row", "col"), None), P(("col", "row"), None), P(), P(), P())
    return jax.shard_map(body, mesh=mesh, in_specs=in_specs, out_specs=P(), check_vma=False)
```

```python
import functools

import jax
import jax.numpy as jnp
from jax import lax
from jax.experimental import pallas as pl
from jax.experimental.pallas import tpu as pltpu
from jax.sharding import PartitionSpec as P


ITERS = 2
LANES = 128
TALL = 512
BOTH = ("row", "col")
SEQUENCE = (2, 4, 3, 7, 6, 1, 0, 5)
NT = (((1,), (1,)), ((), ()))
TN = (((0,), (0,)), ((), ()))
VMEM = pl.BlockSpec(memory_space=pltpu.VMEM)
SMEM = pl.BlockSpec(memory_space=pltpu.SMEM)
HBM = pl.BlockSpec(memory_space=pltpu.HBM)


def sent_to_all(shard, axis):
    peers = lax.axis_size(axis)
    return lax.all_to_all(
        jnp.broadcast_to(shard[None], (peers, *shard.shape)), axis, 0, 0, tiled=True
    )


def place_kernel(axis, order, held_ref, out_ref):
    mine, tall = lax.axis_index(axis), held_ref.shape[1]
    for m, k in enumerate(order):
        start = pl.multiple_of(jnp.bitwise_xor(mine, m) * tall, tall)
        out_ref[pl.ds(start, tall), :] = held_ref[k]


def gathered_by_hops(source, shard, axis, masks):
    peers = lax.axis_size(axis)
    held, known = shard[None], [0]
    for stage, mask in enumerate(masks):
        sent = held if stage else source[None]
        other = lax.ppermute(sent, axis, [(i, i ^ mask) for i in range(peers)])
        held = jnp.concatenate([held, other], 0)
        known = known + [k ^ mask for k in known]
    order = [known.index(m) for m in range(peers)]
    return pl.pallas_call(
        functools.partial(place_kernel, axis, order),
        out_shape=jax.ShapeDtypeStruct((peers * shard.shape[0], shard.shape[1]), shard.dtype),
        in_specs=[VMEM],
        out_specs=VMEM,
        compiler_params=pltpu.CompilerParams(vmem_limit_bytes=4 << 20),
    )(held)


def gathered_by_rows(copies):
    cols = lax.axis_size("col")
    groups = [[row * cols + col for row in SEQUENCE] for col in range(cols)]
    return lax.all_to_all(copies, BOTH, 0, 0, tiled=True, axis_index_groups=groups)


def stage_kernel(
    virt_ref, occ_ref, rhs_ref, e_occ_ref, e_virt_ref,
    copies_ref, occ_out_ref, amp_ref, rhs_mine_ref, denom_mine_ref,
    virt_here, rhs_here, e_occ_here, e_virt_here, denom_here, sem_in, sem_out,
):
    pairs = (
        (virt_ref, virt_here),
        (rhs_ref, rhs_here),
        (e_occ_ref, e_occ_here),
        (e_virt_ref, e_virt_here),
        (occ_ref, occ_out_ref),
    )
    fetches = [pltpu.make_async_copy(*pair, sem_in.at[i]) for i, pair in enumerate(pairs)]
    for fetch in fetches:
        fetch.start()
    fetches[0].wait()
    sends = [
        pltpu.make_async_copy(virt_here, copies_ref.at[peer], sem_out.at[peer])
        for peer in range(copies_ref.shape[0])
    ]
    for send in sends:
        send.start()
    for fetch in fetches[1:]:
        fetch.wait()
    denom = e_virt_here[...] - e_occ_here[...].T
    denom_here[...] = denom
    amp_ref[...] = (rhs_here[...] / denom).astype(amp_ref.dtype)
    tall, lanes = denom_mine_ref.shape
    parts = rhs_here.shape[1] // lanes
    mine = lax.axis_index("row") * lax.axis_size("col") + lax.axis_index("col")
    group, part = mine // parts, mine % parts
    rows = pl.ds(pl.multiple_of(group // 2 * (2 * tall), 2 * tall), 2 * tall)
    columns = pl.ds(pl.multiple_of(part * lanes, lanes), lanes)
    for from_ref, to_ref in ((rhs_here, rhs_mine_ref), (denom_here, denom_mine_ref)):
        pair = from_ref[rows, columns]
        to_ref[...] = jnp.where(group % 2 == 0, pair[:tall], pair[tall:])
    for send in sends:
        send.wait()


def staged(virt, occ, rhs, e_occ, e_virt, tall):
    f32, b16 = jnp.float32, jnp.bfloat16
    peers = lax.axis_size("row")
    small = jax.ShapeDtypeStruct((tall, LANES), f32)
    args = [
        pltpu.with_memory_space_constraint(array, pltpu.HBM)
        for array in (virt, occ, rhs, e_occ.reshape(1, -1), e_virt.reshape(1, -1))
    ]
    return pl.pallas_call(
        stage_kernel,
        out_shape=(
            jax.ShapeDtypeStruct((peers, *virt.shape), b16),
            jax.ShapeDtypeStruct(occ.shape, b16),
            jax.ShapeDtypeStruct(rhs.shape, b16),
            small,
            small,
        ),
        in_specs=[HBM] * 5,
        out_specs=(HBM, VMEM, VMEM, VMEM, VMEM),
        scratch_shapes=[
            pltpu.VMEM(virt.shape, b16),
            pltpu.VMEM(rhs.shape, f32),
            pltpu.VMEM((1, rhs.shape[0]), f32),
            pltpu.VMEM((1, rhs.shape[1]), f32),
            pltpu.VMEM(rhs.shape, f32),
            pltpu.SemaphoreType.DMA((5,)),
            pltpu.SemaphoreType.DMA((peers,)),
        ],
        compiler_params=pltpu.CompilerParams(vmem_limit_bytes=4 << 20),
    )(*args)


def head_kernel(kern_ref, head_ref, sem):
    copy = pltpu.make_async_copy(kern_ref.at[pl.ds(0, head_ref.shape[0])], head_ref, sem)
    copy.start()
    copy.wait()


def head_of(kernel):
    return pl.pallas_call(
        head_kernel,
        out_shape=jax.ShapeDtypeStruct((TALL, kernel.shape[1]), kernel.dtype),
        in_specs=[HBM],
        out_specs=VMEM,
        scratch_shapes=[pltpu.SemaphoreType.DMA],
        compiler_params=pltpu.CompilerParams(vmem_limit_bytes=1 << 20),
    )(pltpu.with_memory_space_constraint(kernel, pltpu.HBM))


def put_together(blocks_ref, out_ref):
    count, tall, lanes = blocks_ref.shape
    parts = out_ref.shape[1] // lanes
    for block in range(count):
        row, column = block // parts * tall, block % parts * lanes
        out_ref[row : row + tall, column : column + lanes] = blocks_ref[block].astype(out_ref.dtype)


def last_kernel(blocks_ref, rhs_ref, e_occ_ref, e_virt_ref, out_ref, exchange_ref):
    put_together(blocks_ref, exchange_ref)
    denom = e_virt_ref[...] - e_occ_ref[...].T
    out_ref[...] = (rhs_ref[...] - exchange_ref[...]) / denom


def last_amplitudes(blocks, rhs, e_occ, e_virt):
    return pl.pallas_call(
        last_kernel,
        out_shape=jax.ShapeDtypeStruct(rhs.shape, jnp.float32),
        in_specs=[VMEM] * 4,
        scratch_shapes=[pltpu.VMEM(rhs.shape, jnp.float32)],
        compiler_params=pltpu.CompilerParams(vmem_limit_bytes=4 << 20),
    )(blocks, rhs, e_occ.reshape(1, -1), e_virt.reshape(1, -1))


def response_kernel(cuts, amp_ref, virt_ref, occ_ref, head_ref, kern_ref, out_ref, *held):
    f32, b16 = jnp.float32, jnp.bfloat16
    tall = head_ref.shape[0]
    blocks = occ_ref.shape[0] // tall
    waits = {}
    if cuts:
        rest_ref, ordered_ref, sem = held
        for i, (first, last) in enumerate(zip(cuts, (*cuts[1:], blocks))):
            size = (last - first) * tall
            waits[first] = pltpu.make_async_copy(
                kern_ref.at[pl.ds(first * tall, size)],
                rest_ref.at[pl.ds((first - 1) * tall, size)],
                sem.at[i],
            )
            waits[first].start()
        share = virt_ref.shape[1]
        for i, row in enumerate(SEQUENCE):
            ordered_ref[row * share : (row + 1) * share, :] = virt_ref[i]
        kern_ref, virt_ref = rest_ref, ordered_ref
    else:
        (joined_ref,) = held
        put_together(amp_ref, joined_ref)
        amp_ref = joined_ref
    w = lax.dot_general(amp_ref[...], virt_ref[...], NT, preferred_element_type=f32).astype(b16)

    def outer_of(block):
        return jnp.dot(occ_ref[pl.ds(block * tall, tall), :], w, preferred_element_type=f32)

    ahead, contracted = outer_of(0), None
    for block in range(blocks):
        here = pl.ds(block * tall, tall)
        if block in waits:
            waits[block].wait()
        outer = ahead
        if block + 1 < blocks:
            ahead = outer_of(block + 1)
        rows_here = kern_ref[pl.ds((block - 1) * tall, tall), :] if block else head_ref[...]
        weighted = (rows_here.astype(f32) * outer).astype(b16)
        more = lax.dot_general(occ_ref[here, :], weighted, TN, preferred_element_type=f32)
        contracted = more if contracted is None else contracted + more
    high = contracted.astype(b16)
    low = (contracted - high.astype(f32)).astype(b16)
    both = jnp.dot(jnp.concatenate([high, low], 0), virt_ref[...], preferred_element_type=f32)
    exchange = both[: high.shape[0]] + both[high.shape[0] :]
    _, rows, lanes = out_ref.shape
    parts = exchange.shape[1] // lanes
    for group in range(exchange.shape[0] // rows):
        for part in range(parts):
            out_ref[group * parts + part] = exchange[
                group * rows : (group + 1) * rows, part * lanes : (part + 1) * lanes
            ].astype(out_ref.dtype)


def first_exchange(amp_b, virt_blocks, occ_rows, head, kernel, pieces):
    peers, share, virtual = virt_blocks.shape
    cuts, b16 = (1, 3), jnp.bfloat16
    return pl.pallas_call(
        functools.partial(response_kernel, cuts),
        out_shape=(
            jax.ShapeDtypeStruct(pieces, b16),
            jax.ShapeDtypeStruct((kernel.shape[0] - head.shape[0], kernel.shape[1]), b16),
            jax.ShapeDtypeStruct((peers * share, virtual), b16),
        ),
        in_specs=[VMEM, VMEM, VMEM, VMEM, HBM],
        out_specs=(VMEM, VMEM, VMEM),
        scratch_shapes=[pltpu.SemaphoreType.DMA((len(cuts),))],
        compiler_params=pltpu.CompilerParams(vmem_limit_bytes=40 << 20),
    )(amp_b, virt_blocks, occ_rows, head, pltpu.with_memory_space_constraint(kernel, pltpu.HBM))


def next_exchange(amp_blocks, virt_cols, occ_rows, head, rest):
    return pl.pallas_call(
        functools.partial(response_kernel, ()),
        out_shape=jax.ShapeDtypeStruct(amp_blocks.shape, jnp.bfloat16),
        in_specs=[VMEM] * 5,
        out_specs=VMEM,
        scratch_shapes=[pltpu.VMEM((occ_rows.shape[1], virt_cols.shape[1]), jnp.bfloat16)],
        compiler_params=pltpu.CompilerParams(vmem_limit_bytes=40 << 20),
    )(amp_blocks, virt_cols, occ_rows, head, rest)


def body(kernel, occ, virt, rhs, e_occ, e_virt):
    occupied, virtual = rhs.shape
    devices = lax.axis_size(BOTH)
    pieces = (devices, occupied * virtual // (devices * LANES), LANES)
    copies, occ_here, amp_b, rhs_mine, denom_mine = staged(
        virt, occ, rhs, e_occ, e_virt, pieces[1]
    )
    virt_blocks = gathered_by_rows(copies)
    occ_rows = gathered_by_hops(occ, occ_here, "col", (8, 4, 2, 1))
    head = head_of(kernel)

    for step in range(ITERS):
        if step == 0:
            part, rest, virt_cols = first_exchange(
                amp_b, virt_blocks, occ_rows, head, kernel, pieces
            )
        else:
            part = next_exchange(amp_b, virt_cols, occ_rows, head, rest)
        parts = lax.all_to_all(part, BOTH, 0, 0, tiled=True)
        exchange = jnp.sum(parts.astype(jnp.float32), axis=0)
        if step < ITERS - 1:
            amp_mine = (rhs_mine - exchange) / denom_mine
            amp_b = sent_to_all(amp_mine.astype(jnp.bfloat16), BOTH)
    return last_amplitudes(sent_to_all(exchange.astype(jnp.bfloat16), BOTH), rhs, e_occ, e_virt)


def solution(mesh):
    in_specs = (P("row", "col"), P(("row", "col"), None), P(("col", "row"), None), P(), P(), P())
    return jax.shard_map(body, mesh=mesh, in_specs=in_specs, out_specs=P(), check_vma=False)
```
